32 devices in a mesh: dp: 8 (over z, x), mp: 4 (over y, core).
Axes of the slice: x: 2, y: 2, z: 4, core: 2. Of those that a mesh axis runs over, the one named last changes fastest.
Arguments:
- patches: bfloat16 [9216, 3072], P('dp'), may hold values from -6 to 6
- weight: bfloat16 [3072, 1536], P(None, 'mp'), may hold values from -0.109375 to 0.109375
- conv_bias: float32 [1536], P('mp'), may hold values from -3 to 3
- cotangent: bfloat16 [9216, 1536], P('dp', 'mp'), may hold values from -0.0390625 to 0.0390625
- row_scale: float32 [3072], replicated, may hold values from 0.25 to 4
- col_scale: float32 [1536], P('mp'), may hold values from 0.25 to 4
Outputs:
- output: bfloat16 [9216, 1536], P('dp', 'mp')
- left_factor: float32 [3072, 3072], P('dp', 'mp')
- right_factor: float32 [1536, 1536], P('dp', 'mp')
- norm_pair: float32 [2], replicated
The draws below stay inside these ranges and needn't reach their ends.
All inputs are finite; a program needn't handle non-finite values.
Results may differ from the reference program's by a relative error of at most 0.001.
Values sent between devices are 32-bit elements; how exact they have to be, the bound alone decides.
A program may use at most 64 MiB of HBM per device.

```python
import math
import jax
import jax.numpy as jnp
from jax import lax

COUT = 1536
K = 3072
ROWS_DEV = 1152
ROWS = 9216
N_DP = 8


def draw_cotangent(key, part):
    row_index = jnp.arange(ROWS).astype(jnp.float32)
    row_ramp = ((1.0 + 2.0 * row_index / (ROWS - 1)) * 0.5 * ROWS ** (-0.5))[:, None]
    first_key = jax.random.fold_in(key, 0)
    third_key = jax.random.fold_in(key, 2)
    edge_value = 3.75 * ROWS ** (-0.5)
    edge_signs = jnp.where(jax.random.uniform(third_key, (1, COUT), jnp.float32) < 0.5, -1.0, 1.0)
    values = jnp.clip(jax.random.normal(first_key, (ROWS, COUT), jnp.float32), -4.9, 4.9) * row_ramp
    values = jnp.clip(values, -edge_value, edge_value)
    last_row = (row_index == ROWS - 1)[:, None]
    values = jnp.where(last_row, edge_signs * edge_value, values)
    return values.astype(jnp.bfloat16)


def raised(entries, key, source, target, blocks, factor):
    owner, partner = [(jnp.arange(entries.shape[axis_at]) // (entries.shape[axis_at] // blocks)).reshape([-1 if axis == axis_at else 1 for axis in range(entries.ndim)]) for axis_at in (source, target)]
    chosen = jax.random.permutation(key, blocks)[partner]
    strong = (owner == chosen) | (owner == (partner + blocks // 2) % blocks)
    return jnp.where(strong, factor * entries, entries)


def steps_of(rng, extent, shards, smallest, high):
    factor_of, own = 1.0, jax.random.fold_in(rng, 6)
    for axis_at, parts in shards:
        steps = jnp.exp(jax.random.uniform(jax.random.fold_in(own, axis_at), (parts,), jnp.float32, smallest / len(shards), high / len(shards)))
        factor_of = factor_of * jnp.repeat(steps, extent[axis_at] // parts).reshape([-1 if axis == axis_at else 1 for axis in range(len(extent))])
    return factor_of


def scatter_about(stream_key, extent, scale, reach, cuts=(), kind=jnp.bfloat16):
    result = scale * jax.random.normal(stream_key, extent, jnp.float32)
    if cuts:
        result = result * steps_of(stream_key, extent, cuts, -0.22, 0.18)
    return jnp.clip(result, -reach, reach).astype(kind)


def heavy_noise(rng, shape, spread, most, shards, heavy, held_as=jnp.bfloat16):
    drawn = spread * jax.random.normal(rng, shape, jnp.float32)
    if shards:
        drawn = drawn * steps_of(rng, shape, shards, -0.22, 0.18)
    return jnp.clip(raised(drawn, jax.random.fold_in(rng, 3), *heavy), -most, most).astype(held_as)


def setup_inputs(seed: int = 0) -> dict:
    arg_keys = jax.random.split(jax.random.key(seed), 7)
    return {
        "patches": heavy_noise(arg_keys[0], (ROWS, K), 1.0, 6.0, ((0, 8),), (0, 1, 8, 2.0)),
        "weight": scatter_about(arg_keys[1], (K, COUT), K ** -0.5, 0.109375, ((1, 4),)),
        "conv_bias": scatter_about(arg_keys[2], (COUT,), 0.5, 3.0, ((0, 4),), jnp.float32),
        "cotangent": draw_cotangent(jax.random.fold_in(arg_keys[6], 71), 0),
        "row_scale": jnp.clip(jnp.exp(jax.random.uniform(arg_keys[4], (K,), jnp.float32, math.log(0.25), math.log(4.0))), 0.25, 4.0),
        "col_scale": jnp.clip(jnp.exp(math.log(4.0) - 2.7725887 * jax.random.uniform(arg_keys[5], (COUT,), jnp.float32) ** steps_of(arg_keys[5], (COUT,), ((0, 4),), -0.2, 0.2)), 0.25, 4.0),
    }


def reference(patches, weight, conv_bias, cotangent, row_scale, col_scale):
    output = (jnp.dot(patches, weight, preferred_element_type=jnp.float32) + conv_bias).astype(jnp.bfloat16)
    inner_width = patches.shape[1]
    out_cols = cotangent.shape[1]
    patch_blocks = patches.reshape(N_DP, ROWS_DEV, inner_width)
    tangents = cotangent.reshape(N_DP, ROWS_DEV, out_cols)
    scale_grid = row_scale[:, None] * col_scale[None, :]

    def accumulate(running, block_pair):
        grad_sum, small_sum = running
        local_grad = lax.dot_general(block_pair[0], block_pair[1], (((0,), (0,)), ((), ())), preferred_element_type=jnp.float32)
        weighted = local_grad * scale_grid
        return (grad_sum + local_grad, small_sum + jnp.sum(weighted * weighted)), None

    starting = (jnp.zeros((inner_width, out_cols), jnp.float32), jnp.zeros((), jnp.float32))
    (gradient, small_sum), _ = lax.scan(accumulate, starting, (patch_blocks, tangents))
    left_factor = jnp.dot(gradient, gradient.T, precision=lax.Precision.HIGHEST, preferred_element_type=jnp.float32) / COUT
    right_factor = jnp.dot(gradient.T, gradient, precision=lax.Precision.HIGHEST, preferred_element_type=jnp.float32) / K
    weighted = gradient * scale_grid
    large_sum = jnp.sum(weighted * weighted)
    norm_pair = jnp.stack([small_sum, large_sum]) / (K * COUT)
    return output, left_factor, right_factor, norm_pair
```

```python
import functools

import jax
import jax.numpy as jnp
from jax import lax
from jax.experimental import pallas as pl
from jax.experimental.pallas import tpu as pltpu
from jax.sharding import PartitionSpec as P

COUT = 1536
K = 3072
F32 = jnp.float32
BF16 = jnp.bfloat16
MESH = pl.DeviceIdType.MESH
FLIPS = ((0, 0), (0, 1), (1, 0), (1, 1))


def shards(patches, weight, conv_bias, cotangent, row_scale, col_scale):
    output = (jnp.dot(patches, weight, preferred_element_type=jnp.float32) + conv_bias).astype(
        jnp.bfloat16
    )
    inner_width = patches.shape[1]
    strip_rows = inner_width // lax.axis_size("dp")
    local_grad = lax.dot_general(
        patches, cotangent, (((0,), (0,)), ((), ())), preferred_element_type=jnp.float32
    )
    weighted = local_grad * row_scale[:, None] * col_scale[None, :]
    small_sum = jnp.sum(weighted * weighted)
    column = lax.psum(local_grad, "dp")
    rows_here = lax.dynamic_slice_in_dim(column, lax.axis_index("dp") * strip_rows, strip_rows, 0)
    left_part = lax.dot_general(
        rows_here,
        column,
        (((1,), (1,)), ((), ())),
        precision=lax.Precision.HIGHEST,
        preferred_element_type=jnp.float32,
    )
    left_factor = lax.psum_scatter(left_part / COUT, "mp", scatter_dimension=1, tiled=True)
    full_strip = lax.all_gather(rows_here, "mp", axis=1, tiled=True)
    right_factor = lax.psum_scatter(
        lax.dot_general(
            full_strip,
            rows_here,
            (((0,), (0,)), ((), ())),
            precision=lax.Precision.HIGHEST,
            preferred_element_type=jnp.float32,
        )
        / K,
        "dp",
        scatter_dimension=0,
        tiled=True,
    )
    row_part = lax.dynamic_slice_in_dim(row_scale, lax.axis_index("dp") * strip_rows, strip_rows, 0)
    scaled_rows = rows_here * row_part[:, None] * col_scale[None, :]
    large_sum = jnp.sum(scaled_rows * scaled_rows)
    small_total, large_total = lax.psum((small_sum, large_sum), ("dp", "mp"))
    norm_pair = jnp.stack([small_total, large_total]) / (K * COUT)
    return (output, left_factor, right_factor, norm_pair)


def flip(bit, by):
    return 1 - bit if by else bit


def halves(value):
    high = value.astype(BF16)
    return high, (value - high.astype(F32)).astype(BF16)


def dot3(a, b, dims):
    a_high, a_low = a
    b_high, b_low = b
    dot = functools.partial(
        lax.dot_general, dimension_numbers=(dims, ((), ())), preferred_element_type=F32
    )
    return dot(a_high, b_high) + (dot(a_high, b_low) + dot(a_low, b_high))


def kernel(
    patches, weight, bias, cot, row_scale, col_scale, output, left, right, norms,
    grad, got_x, got_z1, got_z2, column, lparts, lcore, ly, bcol, racc, rgot, nown, ngot, fsplit,
    s_x, r_x, s_z1, r_z1, s_z2, r_z2,
    s_gx, r_gx, s_gz1, r_gz1, s_gz2, r_gz2,
    s_lc, r_lc, s_ly, r_ly, s_b1, s_b2, r_b, s_r, r_r, s_n, r_n,
):
    d, m = lax.axis_index("dp"), lax.axis_index("mp")
    x, z0, z1 = d % 2, (d // 2) % 2, d // 4
    z = d // 2
    c, y = m % 2, m // 2
    px = (d + 1 - 2 * x, m)
    pz1 = (d + 2 - 4 * z0, m)
    pz2 = (d + 4 - 8 * z1, m)
    pc = (d, m + 1 - 2 * c)
    py = (d, m + 2 - 4 * y)
    size = got_z2.shape[0]
    half = size // 2

    def zk(k):
        f1, f0 = FLIPS[k]
        return 2 * flip(z1, f1) + flip(z0, f0)

    def strip(k, other):
        at = (zk(k) * 2 + flip(x, other)) * size
        return pl.ds(pl.multiple_of(at, size), size)

    def copy(src, dst, send, recv, to):
        return pltpu.make_async_remote_copy(
            src_ref=src, dst_ref=dst, send_sem=send, recv_sem=recv, device_id=to, device_id_type=MESH
        )

    barrier = pltpu.get_barrier_semaphore()
    for to in (px, pz1, pz2, pc, py):
        pl.semaphore_signal(barrier, inc=1, device_id=to, device_id_type=MESH)
    nown[...] = jnp.zeros_like(nown)
    pl.semaphore_wait(barrier, 5)

    def folded(value, rows):
        scaled = value * row_scale[rows, :] * col_scale[...]
        return jnp.sum((scaled * scaled).reshape(-1, 8, value.shape[1]), axis=0)

    def make_grad(rows):
        value = lax.dot_general(
            patches[:, rows], cot[...], (((0,), (0,)), ((), ())), preferred_element_type=F32
        )
        grad[rows, :] = value
        nown[0, 0:8, :] += folded(value, rows)

    ORDER = (3, 2, 1, 0)
    xc = [copy(grad.at[strip(k, 1)], got_x.at[k], s_x.at[k], r_x.at[k], px) for k in range(4)]
    for k in ORDER:
        make_grad(strip(k, 1))
        xc[k].start()
    for k in ORDER:
        make_grad(strip(k, 0))

    def out_tile(i, _):
        rows = pl.ds(pl.multiple_of(i * 128, 128), 128)
        value = jnp.dot(patches[rows, :], weight[...], preferred_element_type=F32) + bias[...]
        output[rows, :] = value.astype(BF16)
        return 0

    def out_tiles(a, b):
        lax.fori_loop(a, b, out_tile, 0)

    tiles = patches.shape[0] // 128
    out_tiles(0, tiles // 3)

    z1c = [copy(got_x.at[2 * f + 1], got_z1.at[f], s_z1.at[f], r_z1.at[f], pz1) for f in range(2)]
    z2c = copy(got_z1.at[1], got_z2, s_z2, r_z2, pz2)
    xc[3].wait_recv()
    got_x[3] += grad[strip(3, 0), :]
    z1c[1].start()
    out_tiles(tiles // 3, 2 * (tiles // 3))
    xc[2].wait_recv()
    got_x[2] += grad[strip(2, 0), :]
    z1c[1].wait_recv()
    got_z1[1] += got_x[2]
    z2c.start()
    out_tiles(2 * (tiles // 3), tiles)
    xc[1].wait_recv()
    got_x[1] += grad[strip(1, 0), :]
    z1c[0].start()
    xc[0].wait_recv()
    got_x[0] += grad[strip(0, 0), :]
    z1c[0].wait_recv()
    got_x[0] += got_z1[0]
    z2c.wait_recv()
    mine = got_x[0] + got_z2[...]
    own = strip(0, 0)
    column[own, :] = mine
    nown[0, 8:16, :] = folded(mine, own)
    high, low = halves(mine)
    fsplit[0] = high
    fsplit[1] = low

    n_to = (px, pz1, pz2, pc, py)
    nc = [copy(nown.at[i], ngot.at[i], s_n.at[i], r_n.at[i], n_to[i]) for i in range(5)]
    nc[0].start()

    def col(k, other):
        return column.at[strip(k, other)]

    gz1 = [copy(col(0, 0), col(0, 0), s_gz1.at[0], r_gz1.at[0], pz1),
           copy(col(2, 0), col(2, 0), s_gz1.at[1], r_gz1.at[1], pz1)]
    gz1_in = [copy(col(1, 0), col(1, 0), s_gz1.at[0], r_gz1.at[0], pz1),
              copy(col(3, 0), col(3, 0), s_gz1.at[1], r_gz1.at[1], pz1)]
    gz2 = copy(col(0, 0), col(0, 0), s_gz2, r_gz2, pz2)
    gz2_in = copy(col(2, 0), col(2, 0), s_gz2, r_gz2, pz2)
    gx = [copy(col(k, 0), col(k, 0), s_gx.at[k], r_gx.at[k], px) for k in range(4)]
    gx_in = [copy(col(k, 1), col(k, 1), s_gx.at[k], r_gx.at[k], px) for k in range(4)]
    lcc = [copy(lparts.at[k], lcore.at[k], s_lc.at[k], r_lc.at[k], pc) for k in range(4)]
    lyc = [copy(lparts.at[k], ly, s_ly, r_ly, py) for k in range(4)]
    b_core = [copy(col(k, 0), bcol.at[k], s_b1.at[k], r_b.at[k], pc) for k in range(4)]
    b_y = [copy(col(k, 0), bcol.at[k], s_b2.at[k], r_b.at[k], py) for k in range(4)]
    b_on = [copy(bcol.at[k], bcol.at[k], s_b1.at[k], r_b.at[k], pc) for k in range(4)]
    source = m == z
    relay = py[1] == z

    gz2.start()
    gz1[0].start()
    gx[0].start()

    def left_part(k, other):
        first = (fsplit[0], fsplit[1])
        value = dot3(first, halves(column[strip(k, other), :]), ((1,), (1,)))
        at = pl.multiple_of(flip(x, other) * size, size)
        lparts[k, :, pl.ds(at, size)] = value

    for k in range(4):
        if k == 1:
            gz1_in[0].wait_recv()
            gx[1].start()
        if k == 2:
            gz2_in.wait_recv()
            gz1[1].start()
            gx[2].start()
        if k == 3:
            gz1_in[1].wait_recv()
            gx[3].start()

        @pl.when(source)
        def _():
            b_y[k].start()
            b_core[k].start()
            bcol[k] = column[strip(k, 0), :]

        left_part(k, 0)

        @pl.when(jnp.logical_not(source))
        def _():
            b_core[k].wait_recv()

        @pl.when(relay)
        def _():
            b_on[k].start()

        value = dot3(halves(bcol[k]), halves(column[strip(k, 0), :]), ((0,), (0,)))
        if k == 0:
            racc[...] = value
        else:
            racc[...] += value
        if k == 3:
            r_half = pl.ds(pl.multiple_of((1 - x) * half, half), half)
            rc = copy(racc.at[r_half], rgot, s_r, r_r, px)
            rc.start()
        gx_in[k].wait_recv()
        left_part(k, 1)

        @pl.when(zk(k) % 2 != c)
        def _():
            lcc[k].start()

        @pl.when(zk(k) % 2 == c)
        def _():
            lcc[k].wait_recv()
            lparts[k] += lcore[k]

            @pl.when(zk(k) // 2 != y)
            def _():
                lyc[k].start()

        nc[k].wait_recv()
        nown[k + 1] = nown[k] + ngot[k]
        nc[k + 1].start()

    rc.wait_recv()
    right[...] = (racc[pl.ds(pl.multiple_of(x * half, half), half), :] + rgot[...]) * (1.0 / K)
    nc[4].wait_recv()
    both = nown[4] + ngot[4]
    norms[0] = jnp.sum(both[0:8]) / (K * COUT)
    norms[1] = jnp.sum(both[8:16]) / (K * COUT)
    lyc[0].wait_recv()
    kk = 2 * ((z1 + y) % 2) + (z0 + c) % 2
    left[...] = (lparts[kk] + ly[...]) * (1.0 / COUT)

    for one in (*xc, *z1c, z2c, *gz1, gz2, *gx, rc, *nc):
        one.wait_send()
    lyc[0].wait_send()
    for k in range(4):

        @pl.when(zk(k) % 2 != c)
        def _():
            lcc[k].wait_send()

        @pl.when(source)
        def _():
            b_y[k].wait_send()
            b_core[k].wait_send()

        @pl.when(relay)
        def _():
            b_on[k].wait_send()


def fused(patches, weight, conv_bias, cotangent, row_scale, col_scale):
    rows, width = patches.shape
    cols = cotangent.shape[1]
    size = width // 8
    vmem = pl.BlockSpec(memory_space=pltpu.VMEM)
    dma = pltpu.SemaphoreType.DMA
    one, four = dma, dma((4,))
    return pl.pallas_call(
        kernel,
        out_shape=(
            jax.ShapeDtypeStruct((rows, cols), BF16),
            jax.ShapeDtypeStruct((size, width // 4), F32),
            jax.ShapeDtypeStruct((cols // 2, cols), F32),
            jax.ShapeDtypeStruct((2,), F32),
        ),
        in_specs=[vmem] * 6,
        out_specs=(vmem, vmem, vmem, pl.BlockSpec(memory_space=pltpu.SMEM)),
        scratch_shapes=[
            pltpu.VMEM((width, cols), F32),
            pltpu.VMEM((4, size, cols), F32),
            pltpu.VMEM((2, size, cols), F32),
            pltpu.VMEM((size, cols), F32),
            pltpu.VMEM((width, cols), F32),
            pltpu.VMEM((4, size, 2 * size), F32),
            pltpu.VMEM((4, size, 2 * size), F32),
            pltpu.VMEM((size, 2 * size), F32),
            pltpu.VMEM((4, size, cols), F32),
            pltpu.VMEM((cols, cols), F32),
            pltpu.VMEM((cols // 2, cols), F32),
            pltpu.VMEM((5, 16, cols), F32),
            pltpu.VMEM((5, 16, cols), F32),
            pltpu.VMEM((2, size, cols), BF16),
            four, four, dma((2,)), dma((2,)), one, one,
            four, four, dma((2,)), dma((2,)), one, one,
            four, four, one, one, four, four, four, one, one, dma((5,)), dma((5,)),
        ],
        compiler_params=pltpu.CompilerParams(
            collective_id=0, has_side_effects=True, vmem_limit_bytes=60 * 1024 * 1024
        ),
    )(
        patches, weight, conv_bias[None, :], cotangent, row_scale[:, None], col_scale[None, :]
    )


def solution(mesh):
    in_specs = (P("dp", None), P(None, "mp"), P("mp"), P("dp", "mp"), P(), P("mp"))
    out_specs = (P("dp", "mp"), P("dp", "mp"), P("dp", "mp"), P())
    body = fused if (mesh.shape["dp"], mesh.shape["mp"]) == (8, 4) else shards
    return jax.shard_map(body, mesh=mesh, in_specs=in_specs, out_specs=out_specs, check_vma=False)
```

```python
import functools

import jax
import jax.numpy as jnp
from jax import lax
from jax.experimental import pallas as pl
from jax.experimental.pallas import tpu as pltpu
from jax.sharding import PartitionSpec as P

COUT = 1536
K = 3072
F32 = jnp.float32
BF16 = jnp.bfloat16
MESH = pl.DeviceIdType.MESH


def shards(patches, weight, conv_bias, cotangent, row_scale, col_scale):
    output = (jnp.dot(patches, weight, preferred_element_type=jnp.float32) + conv_bias).astype(
        jnp.bfloat16
    )
    inner_width = patches.shape[1]
    strip_rows = inner_width // lax.axis_size("dp")
    local_grad = lax.dot_general(
        patches, cotangent, (((0,), (0,)), ((), ())), preferred_element_type=jnp.float32
    )
    weighted = local_grad * row_scale[:, None] * col_scale[None, :]
    small_sum = jnp.sum(weighted * weighted)
    column = lax.psum(local_grad, "dp")
    rows_here = lax.dynamic_slice_in_dim(column, lax.axis_index("dp") * strip_rows, strip_rows, 0)
    left_part = lax.dot_general(
        rows_here,
        column,
        (((1,), (1,)), ((), ())),
        precision=lax.Precision.HIGHEST,
        preferred_element_type=jnp.float32,
    )
    left_factor = lax.psum_scatter(left_part / COUT, "mp", scatter_dimension=1, tiled=True)
    full_strip = lax.all_gather(rows_here, "mp", axis=1, tiled=True)
    right_factor = lax.psum_scatter(
        lax.dot_general(
            full_strip,
            rows_here,
            (((0,), (0,)), ((), ())),
            precision=lax.Precision.HIGHEST,
            preferred_element_type=jnp.float32,
        )
        / K,
        "dp",
        scatter_dimension=0,
        tiled=True,
    )
    row_part = lax.dynamic_slice_in_dim(row_scale, lax.axis_index("dp") * strip_rows, strip_rows, 0)
    scaled_rows = rows_here * row_part[:, None] * col_scale[None, :]
    large_sum = jnp.sum(scaled_rows * scaled_rows)
    small_total, large_total = lax.psum((small_sum, large_sum), ("dp", "mp"))
    norm_pair = jnp.stack([small_total, large_total]) / (K * COUT)
    return (output, left_factor, right_factor, norm_pair)


def flip(bit, by):
    return 1 - bit if by else bit


def halves(value):
    high = value.astype(BF16)
    return high, (value - high.astype(F32)).astype(BF16)


def dot3(a, b, dims):
    a_high, a_low = a
    b_high, b_low = b
    dot = functools.partial(
        lax.dot_general, dimension_numbers=(dims, ((), ())), preferred_element_type=F32
    )
    return dot(a_high, b_high) + (dot(a_high, b_low) + dot(a_low, b_high))


def kernel(
    patches, weight, rows2, cot, row_scale, output, left, right, norms,
    grad, got_x, got_p, got_i, column, lparts, lcore, ly, bcol, racc, rgot, nown, ngot, fsplit,
    s_x, r_x, s_p, r_p, s_i, r_i,
    s_gx, r_gx, s_gp, s_gi, r_g,
    s_lc, r_lc, s_ly, r_ly, s_b1, s_b2, r_b, s_r, r_r, s_n, r_n,
):
    d, m = lax.axis_index("dp"), lax.axis_index("mp")
    x, z = d % 2, d // 2
    z0, z1 = z % 2, z // 2
    c, y = m % 2, m // 2
    zs = (z, z + 1 - 2 * z0, 2 - z1, 3 - 3 * z1)
    px = (d + 1 - 2 * x, m)
    pz = (zs[1] * 2 + x, m)
    pi = ((3 - z) * 2 + x, m)
    pc = (d, m + 1 - 2 * c)
    py = (d, m + 2 - 4 * y)
    inner = (z0 + z1) % 2 == 1
    outer = (z0 + z1) % 2 == 0
    size = rgot.shape[1]
    half = rgot.shape[0]

    def strip_at(k, other):
        return zs[k] * 2 + (1 - x if other else x)

    def strip(k, other):
        return pl.ds(pl.multiple_of(strip_at(k, other) * size, size), size)

    def copy(src, dst, send, recv, to):
        return pltpu.make_async_remote_copy(
            src_ref=src, dst_ref=dst, send_sem=send, recv_sem=recv, device_id=to, device_id_type=MESH
        )

    barrier = pltpu.get_barrier_semaphore()
    for to in (px, pz, pi, pc, py):
        pl.semaphore_signal(barrier, inc=1, device_id=to, device_id_type=MESH)
    nown[...] = jnp.zeros_like(nown)
    pl.semaphore_wait(barrier, 5)
    bias = rows2[0:1, :]
    col_square = rows2[1:2, :] * rows2[1:2, :]

    def folded(value, at):
        square = value * value * col_square
        total = jnp.zeros((1, size), F32)
        for b in range(size // 128):
            scale = row_scale[pl.ds(at * (size // 128) + b, 1), :]
            total += dot3(
                halves(scale * scale), halves(square[b * 128:(b + 1) * 128]), ((1,), (0,))
            )
        return total

    def make_grad(k, other):
        rows = strip(k, other)
        grad[rows, :] = lax.dot_general(
            patches[:, rows], cot[...], (((0,), (0,)), ((), ())), preferred_element_type=F32
        )

    ORDER = (3, 2, 1, 0)
    xc = [copy(grad.at[strip(k, 1)], got_x.at[k], s_x.at[k], r_x.at[k], px) for k in range(4)]
    for k in ORDER:
        make_grad(k, 1)
        xc[k].start()
    for k in ORDER:
        make_grad(k, 0)

    def small_norm(s, _):
        rows = pl.ds(pl.multiple_of(s * size, size), size)
        nown[0, 0:1, :] += folded(grad[rows, :], s)
        return 0

    lax.fori_loop(0, 8, small_norm, 0)

    def out_tile(i, _):
        rows = pl.ds(pl.multiple_of(i * 128, 128), 128)
        value = jnp.dot(patches[rows, :], weight[...], preferred_element_type=F32) + bias
        output[rows, :] = value.astype(BF16)
        return 0

    def out_tiles(a, b):
        lax.fori_loop(a, b, out_tile, 0)

    tiles = patches.shape[0] // 128
    cuts = [0, tiles // 3, 2 * (tiles // 3), tiles]

    to_p = {
        k: copy(got_x.at[k], got_p.at[k - 1], s_p.at[k - 1], r_p.at[k - 1], pz) for k in (1, 2, 3)
    }
    to_i = {
        k: copy(got_x.at[k], got_i.at[k - 2], s_i.at[k - 2], r_i.at[k - 2], pi) for k in (2, 3)
    }
    for k in ORDER:
        xc[k].wait_recv()
        got_x[k] += grad[strip(k, 0), :]
        if k >= 1:

            @pl.when(outer)
            def _():
                to_p[k].start()

        if k >= 2:

            @pl.when(inner)
            def _():
                to_p[k].wait_recv()
                got_x[k] += got_p[k - 1]
                to_i[k].start()

            out_tiles(cuts[3 - k], cuts[4 - k])
        if k == 1:

            @pl.when(inner)
            def _():
                to_i[3].wait_recv()
                got_x[1] += got_i[1]
                to_p[1].start()

            out_tiles(cuts[2], cuts[3])
    to_p[1].wait_recv()
    got_x[0] += got_p[0]

    @pl.when(inner)
    def _():
        to_i[2].wait_recv()
        got_x[0] += got_i[0]

    own = strip(0, 0)
    column[own, :] = got_x[0]

    def col(k, other):
        return column.at[strip(k, other)]

    def pass_on(k, recv, send, to):
        return copy(col(k, 0), col(k, 0), send, r_g.at[recv], to)

    gp = [pass_on((0, 2, 3)[j], j + 1, s_gp.at[j], pz) for j in range(3)]
    gi = [pass_on(j, j + 2, s_gi.at[j], pi) for j in range(2)]
    g_in = [pass_on(k, k, s_gp.at[0], pz) for k in range(4)]
    gx = [copy(col(k, 0), col(k, 0), s_gx.at[k], r_gx.at[k], px) for k in range(4)]
    gx_in = [copy(col(k, 1), col(k, 1), s_gx.at[k], r_gx.at[k], px) for k in range(4)]
    units = [(k, o) for k in range(4) for o in range(2)]
    lcc = {
        (k, o): copy(
            lparts.at[k, o], lcore.at[k, o], s_lc.at[2 * k + o], r_lc.at[2 * k + o], pc
        )
        for k, o in units
    }
    lyc = {(k, o): copy(lparts.at[k, o], ly.at[o], s_ly.at[o], r_ly.at[o], py) for k, o in units}
    b_core = [copy(col(k, 0), bcol.at[k], s_b1.at[k], r_b.at[k], pc) for k in range(4)]
    b_y = [copy(col(k, 0), bcol.at[k], s_b2.at[k], r_b.at[k], py) for k in range(4)]
    b_on = [copy(bcol.at[k], bcol.at[k], s_b1.at[k], r_b.at[k], pc) for k in range(4)]
    source = m == z
    relay = py[1] == z

    def arrive(k):
        if k >= 1:
            g_in[k].wait_recv()
        gx[k].start()
        if k == 0:
            gp[0].start()

        @pl.when(inner)
        def _():
            if k <= 1:
                gi[k].start()
            else:
                gp[k - 1].start()

        @pl.when(source)
        def _():
            b_y[k].start()
            b_core[k].start()

    arrive(0)
    high, low = halves(got_x[0])
    fsplit[0] = high
    fsplit[1] = low
    nown[0, 8:9, :] = folded(got_x[0], strip_at(0, 0))
    n_to = (px, pz, pi, pc, py)
    nc = [copy(nown.at[i], ngot.at[i], s_n.at[i], r_n.at[i], n_to[i]) for i in range(5)]
    nc[0].start()
    waiting = []

    def collect():
        if not waiting:
            return
        k, o = waiting.pop(0)

        @pl.when(zs[k] % 2 == c)
        def _():
            lcc[k, o].wait_recv()
            lparts[k, o] += lcore[k, o]

            @pl.when(zs[k] // 2 != y)
            def _():
                lyc[k, o].start()

    def left_unit(k, o):
        if o:
            gx_in[k].wait_recv()
        lparts[k, o] = dot3((fsplit[0], fsplit[1]), halves(column[strip(k, o), :]), ((1,), (1,)))

        @pl.when(zs[k] % 2 != c)
        def _():
            lcc[k, o].start()

        collect()
        waiting.append((k, o))

    def right_unit(k):
        @pl.when(source)
        def _():
            bcol[k] = column[strip(k, 0), :]

        @pl.when(jnp.logical_not(source))
        def _():
            b_core[k].wait_recv()

        @pl.when(relay)
        def _():
            b_on[k].start()

        value = dot3(halves(bcol[k]), halves(column[strip(k, 0), :]), ((0,), (0,)))
        if k == 0:
            racc[...] = value
        else:
            racc[...] += value

    def norm_step(i):
        nc[i].wait_recv()
        nown[i + 1] = nown[i] + ngot[i]
        nc[i + 1].start()

    left_unit(0, 0)
    for k in range(1, 4):
        arrive(k)
        left_unit(k, 0)
        left_unit(k - 1, 1)
        collect()
        right_unit(k - 1)
        norm_step(k - 1)
    left_unit(3, 1)
    collect()
    right_unit(3)
    rc = copy(
        racc.at[pl.ds(pl.multiple_of((1 - x) * half, half), half)], rgot, s_r, r_r, px
    )
    rc.start()
    norm_step(3)
    nc[4].wait_recv()
    both = nown[4] + ngot[4]
    norms[0] = jnp.sum(both[0:8]) / (K * COUT)
    norms[1] = jnp.sum(both[8:16]) / (K * COUT)
    at_k = 0
    for k in range(1, 4):
        at_k = at_k + k * (zs[k] == m).astype(jnp.int32)
    for o in range(2):
        lyc[0, o].wait_recv()
        at = pl.multiple_of((1 - x if o else x) * size, size)
        left[:, pl.ds(at, size)] = (lparts[at_k, o] + ly[o]) * (1.0 / COUT)
    rc.wait_recv()
    right[...] = (racc[pl.ds(pl.multiple_of(x * half, half), half), :] + rgot[...]) * (1.0 / K)

    for one in (*xc, to_p[1], gp[0], *gx, rc, *nc, lyc[0, 0], lyc[0, 1]):
        one.wait_send()

    @pl.when(outer)
    def _():
        to_p[2].wait_send()
        to_p[3].wait_send()

    @pl.when(inner)
    def _():
        for one in (to_i[2], to_i[3], gp[1], gp[2], *gi):
            one.wait_send()

    for k in range(4):

        @pl.when(zs[k] % 2 != c)
        def _():
            lcc[k, 0].wait_send()
            lcc[k, 1].wait_send()

        @pl.when(source)
        def _():
            b_y[k].wait_send()
            b_core[k].wait_send()

        @pl.when(relay)
        def _():
            b_on[k].wait_send()


def fused(patches, weight, conv_bias, cotangent, row_scale, col_scale):
    rows, width = patches.shape
    cols = cotangent.shape[1]
    size = width // 8
    vmem = pl.BlockSpec(memory_space=pltpu.VMEM)
    dma = pltpu.SemaphoreType.DMA
    one, four = dma, dma((4,))
    return pl.pallas_call(
        kernel,
        out_shape=(
            jax.ShapeDtypeStruct((rows, cols), BF16),
            jax.ShapeDtypeStruct((size, width // 4), F32),
            jax.ShapeDtypeStruct((cols // 2, cols), F32),
            jax.ShapeDtypeStruct((2,), F32),
        ),
        in_specs=[vmem] * 5,
        out_specs=(vmem, vmem, vmem, pl.BlockSpec(memory_space=pltpu.SMEM)),
        scratch_shapes=[
            pltpu.VMEM((width, cols), F32),
            pltpu.VMEM((4, size, cols), F32),
            pltpu.VMEM((3, size, cols), F32),
            pltpu.VMEM((2, size, cols), F32),
            pltpu.VMEM((width, cols), F32),
            pltpu.VMEM((4, 2, size, size), F32),
            pltpu.VMEM((4, 2, size, size), F32),
            pltpu.VMEM((2, size, size), F32),
            pltpu.VMEM((4, size, cols), F32),
            pltpu.VMEM((cols, cols), F32),
            pltpu.VMEM((cols // 2, cols), F32),
            pltpu.VMEM((5, 16, cols), F32),
            pltpu.VMEM((5, 16, cols), F32),
            pltpu.VMEM((2, size, cols), BF16),
            four, four, dma((3,)), dma((3,)), dma((2,)), dma((2,)),
            four, four, dma((3,)), dma((2,)), four,
            dma((8,)), dma((8,)), dma((2,)), dma((2,)), four, four, four, one, one,
            dma((5,)), dma((5,)),
        ],
        compiler_params=pltpu.CompilerParams(
            collective_id=0, has_side_effects=True, vmem_limit_bytes=60 * 1024 * 1024
        ),
    )(
        patches, weight, jnp.stack([conv_bias, col_scale]), cotangent, row_scale.reshape(-1, 128)
    )


def solution(mesh):
    in_specs = (P("dp", None), P(None, "mp"), P("mp"), P("dp", "mp"), P(), P("mp"))
    out_specs = (P("dp", "mp"), P("dp", "mp"), P("dp", "mp"), P())
    body = fused if (mesh.shape["dp"], mesh.shape["mp"]) == (8, 4) else shards
    return jax.shard_map(body, mesh=mesh, in_specs=in_specs, out_specs=out_specs, check_vma=False)
```

```python
import functools

import jax
import jax.numpy as jnp
from jax import lax
from jax.experimental import pallas as pl
from jax.experimental.pallas import tpu as pltpu
from jax.sharding import PartitionSpec as P

COUT = 1536
K = 3072
F32 = jnp.float32
BF16 = jnp.bfloat16
MESH = pl.DeviceIdType.MESH


def shards(patches, weight, conv_bias, cotangent, row_scale, col_scale):
    output = (jnp.dot(patches, weight, preferred_element_type=jnp.float32) + conv_bias).astype(
        jnp.bfloat16
    )
    inner_width = patches.shape[1]
    strip_rows = inner_width // lax.axis_size("dp")
    local_grad = lax.dot_general(
        patches, cotangent, (((0,), (0,)), ((), ())), preferred_element_type=jnp.float32
    )
    weighted = local_grad * row_scale[:, None] * col_scale[None, :]
    small_sum = jnp.sum(weighted * weighted)
    column = lax.psum(local_grad, "dp")
    rows_here = lax.dynamic_slice_in_dim(column, lax.axis_index("dp") * strip_rows, strip_rows, 0)
    left_part = lax.dot_general(
        rows_here,
        column,
        (((1,), (1,)), ((), ())),
        precision=lax.Precision.HIGHEST,
        preferred_element_type=jnp.float32,
    )
    left_factor = lax.psum_scatter(left_part / COUT, "mp", scatter_dimension=1, tiled=True)
    full_strip = lax.all_gather(rows_here, "mp", axis=1, tiled=True)
    right_factor = lax.psum_scatter(
        lax.dot_general(
            full_strip,
            rows_here,
            (((0,), (0,)), ((), ())),
            precision=lax.Precision.HIGHEST,
            preferred_element_type=jnp.float32,
        )
        / K,
        "dp",
        scatter_dimension=0,
        tiled=True,
    )
    row_part = lax.dynamic_slice_in_dim(row_scale, lax.axis_index("dp") * strip_rows, strip_rows, 0)
    scaled_rows = rows_here * row_part[:, None] * col_scale[None, :]
    large_sum = jnp.sum(scaled_rows * scaled_rows)
    small_total, large_total = lax.psum((small_sum, large_sum), ("dp", "mp"))
    norm_pair = jnp.stack([small_total, large_total]) / (K * COUT)
    return (output, left_factor, right_factor, norm_pair)


def flip(bit, by):
    return 1 - bit if by else bit


def halves(value):
    high = value.astype(BF16)
    return high, (value - high.astype(F32)).astype(BF16)


def dot3(a, b, dims):
    a_high, a_low = a
    b_high, b_low = b
    dot = functools.partial(
        lax.dot_general, dimension_numbers=(dims, ((), ())), preferred_element_type=F32
    )
    return dot(a_high, b_high) + (dot(a_high, b_low) + dot(a_low, b_high))


def kernel(
    patches_in, weight_in, bias_in, cot, row_scale, col_scale, output_out, left, right, norms,
    grad, got_x, got_p, got_i, column, lparts, lcore, ly, bcol, racc, rgot, nown, ngot, fsplit,
    s_x, r_x, s_p, r_p, s_i, r_i,
    s_gx, r_gx, s_gp, s_gi, r_g,
    s_lc, r_lc, s_ly, r_ly, s_b1, s_b2, r_b, s_r, r_r, s_n, r_n,
    patches, weight, output, load, w_load, o_store,
):
    d, m = lax.axis_index("dp"), lax.axis_index("mp")
    x, z = d % 2, d // 2
    z0, z1 = z % 2, z // 2
    c, y = m % 2, m // 2
    zs = (z, z + 1 - 2 * z0, 2 - z1, 3 - 3 * z1)
    px = (d + 1 - 2 * x, m)
    pz = (zs[1] * 2 + x, m)
    pi = ((3 - z) * 2 + x, m)
    pc = (d, m + 1 - 2 * c)
    py = (d, m + 2 - 4 * y)
    inner = (z0 + z1) % 2 == 1
    outer = (z0 + z1) % 2 == 0
    size = rgot.shape[1]
    half = rgot.shape[0]

    def strip_at(k, other):
        return zs[k] * 2 + (1 - x if other else x)

    def strip(k, other):
        return pl.ds(pl.multiple_of(strip_at(k, other) * size, size), size)

    def copy(src, dst, send, recv, to):
        return pltpu.make_async_remote_copy(
            src_ref=src, dst_ref=dst, send_sem=send, recv_sem=recv, device_id=to, device_id_type=MESH
        )

    barrier = pltpu.get_barrier_semaphore()
    for to in (px, pz, pi, pc, py):
        pl.semaphore_signal(barrier, inc=1, device_id=to, device_id_type=MESH)
    ORDER = (3, 2, 1, 0)
    loads = {}
    for o in (1, 0):
        for k in ORDER:
            rows = strip(k, o)
            loads[k, o] = pltpu.make_async_copy(
                patches_in.at[:, rows], patches.at[:, rows], load.at[2 * k + o]
            )
            loads[k, o].start()
    weight_load = pltpu.make_async_copy(weight_in, weight, w_load)
    weight_load.start()
    nown[...] = jnp.zeros_like(nown)
    pl.semaphore_wait(barrier, 5)
    bias = bias_in[...].reshape(1, size)
    col_row = col_scale[...].reshape(1, size)
    col_square = col_row * col_row

    def folded(value, at):
        square = value * value * col_square
        total = jnp.zeros((1, size), F32)
        for b in range(size // 128):
            scale = row_scale[pl.ds(at * (size // 128) + b, 1), :]
            total += dot3(
                halves(scale * scale), halves(square[b * 128:(b + 1) * 128]), ((1,), (0,))
            )
        return total

    def make_grad(k, other):
        rows = strip(k, other)
        loads[k, other].wait()
        grad[rows, :] = lax.dot_general(
            patches[:, rows], cot[...], (((0,), (0,)), ((), ())), preferred_element_type=F32
        )

    xc = [copy(grad.at[strip(k, 1)], got_x.at[k], s_x.at[k], r_x.at[k], px) for k in range(4)]
    for k in ORDER:
        make_grad(k, 1)
        xc[k].start()
    for k in ORDER:
        make_grad(k, 0)

    weight_load.wait()

    def small_norm(s, _):
        rows = pl.ds(pl.multiple_of(s * size, size), size)
        nown[0, 0:1, :] += folded(grad[rows, :], s)
        return 0

    lax.fori_loop(0, 8, small_norm, 0)

    def out_tile(i, _):
        rows = pl.ds(pl.multiple_of(i * 128, 128), 128)
        value = jnp.dot(patches[rows, :], weight[...], preferred_element_type=F32) + bias
        output[rows, :] = value.astype(BF16)
        return 0

    def out_tiles(a, b):
        lax.fori_loop(a, b, out_tile, 0)

    tiles = patches.shape[0] // 128
    cuts = [0, tiles // 3, 2 * (tiles // 3), tiles]

    to_p = {
        k: copy(got_x.at[k], got_p.at[k - 1], s_p.at[k - 1], r_p.at[k - 1], pz) for k in (1, 2, 3)
    }
    to_i = {
        k: copy(got_x.at[k], got_i.at[k - 2], s_i.at[k - 2], r_i.at[k - 2], pi) for k in (2, 3)
    }
    for k in ORDER:
        xc[k].wait_recv()
        got_x[k] += grad[strip(k, 0), :]
        if k >= 1:

            @pl.when(outer)
            def _():
                to_p[k].start()

        if k >= 2:

            @pl.when(inner)
            def _():
                to_p[k].wait_recv()
                got_x[k] += got_p[k - 1]
                to_i[k].start()

            out_tiles(cuts[3 - k], cuts[4 - k])
        if k == 1:

            @pl.when(inner)
            def _():
                to_i[3].wait_recv()
                got_x[1] += got_i[1]
                to_p[1].start()

            out_tiles(cuts[2], cuts[3])
            out_copy = pltpu.make_async_copy(output, output_out, o_store)
            out_copy.start()
    to_p[1].wait_recv()
    got_x[0] += got_p[0]

    @pl.when(inner)
    def _():
        to_i[2].wait_recv()
        got_x[0] += got_i[0]

    own = strip(0, 0)
    column[own, :] = got_x[0]

    def col(k, other):
        return column.at[strip(k, other)]

    def pass_on(k, recv, send, to):
        return copy(col(k, 0), col(k, 0), send, r_g.at[recv], to)

    gp = [pass_on((0, 2, 3)[j], j + 1, s_gp.at[j], pz) for j in range(3)]
    gi = [pass_on(j, j + 2, s_gi.at[j], pi) for j in range(2)]
    g_in = [pass_on(k, k, s_gp.at[0], pz) for k in range(4)]
    gx = [copy(col(k, 0), col(k, 0), s_gx.at[k], r_gx.at[k], px) for k in range(4)]
    gx_in = [copy(col(k, 1), col(k, 1), s_gx.at[k], r_gx.at[k], px) for k in range(4)]
    units = [(k, o) for k in range(4) for o in range(2)]
    lcc = {
        (k, o): copy(
            lparts.at[k, o], lcore.at[k, o], s_lc.at[2 * k + o], r_lc.at[2 * k + o], pc
        )
        for k, o in units
    }
    lyc = {(k, o): copy(lparts.at[k, o], ly.at[o], s_ly.at[o], r_ly.at[o], py) for k, o in units}
    b_core = [copy(col(k, 0), bcol.at[k], s_b1.at[k], r_b.at[k], pc) for k in range(4)]
    b_y = [copy(col(k, 0), bcol.at[k], s_b2.at[k], r_b.at[k], py) for k in range(4)]
    b_on = [copy(bcol.at[k], bcol.at[k], s_b1.at[k], r_b.at[k], pc) for k in range(4)]
    source = m == z
    relay = py[1] == z

    def arrive(k):
        if k >= 1:
            g_in[k].wait_recv()
        gx[k].start()
        if k == 0:
            gp[0].start()

        @pl.when(inner)
        def _():
            if k <= 1:
                gi[k].start()
            else:
                gp[k - 1].start()

        @pl.when(source)
        def _():
            b_y[k].start()
            b_core[k].start()

    arrive(0)
    high, low = halves(got_x[0])
    fsplit[0] = high
    fsplit[1] = low
    nown[0, 8:9, :] = folded(got_x[0], strip_at(0, 0))
    n_to = (pc, py, pz, pi, px)
    nc = [copy(nown.at[i], ngot.at[i], s_n.at[i], r_n.at[i], n_to[i]) for i in range(5)]
    nc[0].start()
    waiting = []

    def collect():
        if not waiting:
            return
        k, o = waiting.pop(0)

        @pl.when(zs[k] % 2 == c)
        def _():
            lcc[k, o].wait_recv()
            lparts[k, o] += lcore[k, o]

            @pl.when(zs[k] // 2 != y)
            def _():
                lyc[k, o].start()

    def left_unit(k, o):
        if o:
            gx_in[k].wait_recv()
        lparts[k, o] = dot3((fsplit[0], fsplit[1]), halves(column[strip(k, o), :]), ((1,), (1,)))

        @pl.when(zs[k] % 2 != c)
        def _():
            lcc[k, o].start()

        collect()
        waiting.append((k, o))

    def right_unit(k):
        @pl.when(source)
        def _():
            bcol[k] = column[strip(k, 0), :]

        @pl.when(jnp.logical_not(source))
        def _():
            b_core[k].wait_recv()

        @pl.when(relay)
        def _():
            b_on[k].start()

        value = dot3(halves(bcol[k]), halves(column[strip(k, 0), :]), ((0,), (0,)))
        if k == 0:
            racc[...] = value
        else:
            racc[...] += value

    def norm_step(i):
        nc[i].wait_recv()
        nown[i + 1] = nown[i] + ngot[i]
        nc[i + 1].start()

    left_unit(0, 0)
    for k in range(1, 4):
        arrive(k)
        left_unit(k, 0)
        left_unit(k - 1, 1)
        collect()
        right_unit(k - 1)
        norm_step(k - 1)
    left_unit(3, 1)
    norm_step(3)
    right_unit(3)
    rc = copy(
        racc.at[pl.ds(pl.multiple_of((1 - x) * half, half), half)], rgot, s_r, r_r, px
    )
    rc.start()
    collect()
    nc[4].wait_recv()
    both = nown[4] + ngot[4]
    norms[0] = jnp.sum(both[0:8]) / (K * COUT)
    norms[1] = jnp.sum(both[8:16]) / (K * COUT)
    at_k = 0
    for k in range(1, 4):
        at_k = at_k + k * (zs[k] == m).astype(jnp.int32)
    for o in range(2):
        lyc[0, o].wait_recv()
        at = pl.multiple_of((1 - x if o else x) * size, size)
        left[:, pl.ds(at, size)] = (lparts[at_k, o] + ly[o]) * (1.0 / COUT)
    rc.wait_recv()
    right[...] = (racc[pl.ds(pl.multiple_of(x * half, half), half), :] + rgot[...]) * (1.0 / K)

    out_copy.wait()
    for one in (*xc, to_p[1], gp[0], *gx, rc, *nc, lyc[0, 0], lyc[0, 1]):
        one.wait_send()

    @pl.when(outer)
    def _():
        to_p[2].wait_send()
        to_p[3].wait_send()

    @pl.when(inner)
    def _():
        for one in (to_i[2], to_i[3], gp[1], gp[2], *gi):
            one.wait_send()

    for k in range(4):

        @pl.when(zs[k] % 2 != c)
        def _():
            lcc[k, 0].wait_send()
            lcc[k, 1].wait_send()

        @pl.when(source)
        def _():
            b_y[k].wait_send()
            b_core[k].wait_send()

        @pl.when(relay)
        def _():
            b_on[k].wait_send()


def fused(patches, weight, conv_bias, cotangent, row_scale, col_scale):
    rows, width = patches.shape
    cols = cotangent.shape[1]
    size = width // 8
    vmem = pl.BlockSpec(memory_space=pltpu.VMEM)
    hbm = pl.BlockSpec(memory_space=pl.ANY)
    dma = pltpu.SemaphoreType.DMA
    one, four = dma, dma((4,))
    return pl.pallas_call(
        kernel,
        out_shape=(
            jax.ShapeDtypeStruct((rows, cols), BF16),
            jax.ShapeDtypeStruct((size, width // 4), F32),
            jax.ShapeDtypeStruct((cols // 2, cols), F32),
            jax.ShapeDtypeStruct((2,), F32),
        ),
        in_specs=[hbm, hbm, vmem, vmem, vmem, vmem],
        out_specs=(hbm, vmem, vmem, pl.BlockSpec(memory_space=pltpu.SMEM)),
        scratch_shapes=[
            pltpu.VMEM((width, cols), F32),
            pltpu.VMEM((4, size, cols), F32),
            pltpu.VMEM((3, size, cols), F32),
            pltpu.VMEM((2, size, cols), F32),
            pltpu.VMEM((width, cols), F32),
            pltpu.VMEM((4, 2, size, size), F32),
            pltpu.VMEM((4, 2, size, size), F32),
            pltpu.VMEM((2, size, size), F32),
            pltpu.VMEM((4, size, cols), F32),
            pltpu.VMEM((cols, cols), F32),
            pltpu.VMEM((cols // 2, cols), F32),
            pltpu.VMEM((5, 16, cols), F32),
            pltpu.VMEM((5, 16, cols), F32),
            pltpu.VMEM((2, size, cols), BF16),
            four, four, dma((3,)), dma((3,)), dma((2,)), dma((2,)),
            four, four, dma((3,)), dma((2,)), four,
            dma((8,)), dma((8,)), dma((2,)), dma((2,)), four, four, four, one, one,
            dma((5,)), dma((5,)),
            pltpu.VMEM((rows, width), BF16),
            pltpu.VMEM((width, cols), BF16),
            pltpu.VMEM((rows, cols), BF16),
            dma((8,)), one, one,
        ],
        compiler_params=pltpu.CompilerParams(
            collective_id=0, has_side_effects=True, vmem_limit_bytes=60 * 1024 * 1024
        ),
    )(
        patches, weight, conv_bias, cotangent, row_scale.reshape(-1, 128), col_scale
    )


def solution(mesh):
    in_specs = (P("dp", None), P(None, "mp"), P("mp"), P("dp", "mp"), P(), P("mp"))
    out_specs = (P("dp", "mp"), P("dp", "mp"), P("dp", "mp"), P())
    body = fused if (mesh.shape["dp"], mesh.shape["mp"]) == (8, 4) else shards
    return jax.shard_map(body, mesh=mesh, in_specs=in_specs, out_specs=out_specs, check_vma=False)
```

```python
import functools

import jax
import jax.numpy as jnp
from jax import lax
from jax.experimental import pallas as pl
from jax.experimental.pallas import tpu as pltpu
from jax.sharding import PartitionSpec as P

COUT = 1536
K = 3072
F32 = jnp.float32
BF16 = jnp.bfloat16
MESH = pl.DeviceIdType.MESH


def shards(patches, weight, conv_bias, cotangent, row_scale, col_scale):
    output = (jnp.dot(patches, weight, preferred_element_type=jnp.float32) + conv_bias).astype(
        jnp.bfloat16
    )
    inner_width = patches.shape[1]
    strip_rows = inner_width // lax.axis_size("dp")
    local_grad = lax.dot_general(
        patches, cotangent, (((0,), (0,)), ((), ())), preferred_element_type=jnp.float32
    )
    weighted = local_grad * row_scale[:, None] * col_scale[None, :]
    small_sum = jnp.sum(weighted * weighted)
    column = lax.psum(local_grad, "dp")
    rows_here = lax.dynamic_slice_in_dim(column, lax.axis_index("dp") * strip_rows, strip_rows, 0)
    left_part = lax.dot_general(
        rows_here,
        column,
        (((1,), (1,)), ((), ())),
        precision=lax.Precision.HIGHEST,
        preferred_element_type=jnp.float32,
    )
    left_factor = lax.psum_scatter(left_part / COUT, "mp", scatter_dimension=1, tiled=True)
    full_strip = lax.all_gather(rows_here, "mp", axis=1, tiled=True)
    right_factor = lax.psum_scatter(
        lax.dot_general(
            full_strip,
            rows_here,
            (((0,), (0,)), ((), ())),
            precision=lax.Precision.HIGHEST,
            preferred_element_type=jnp.float32,
        )
        / K,
        "dp",
        scatter_dimension=0,
        tiled=True,
    )
    row_part = lax.dynamic_slice_in_dim(row_scale, lax.axis_index("dp") * strip_rows, strip_rows, 0)
    scaled_rows = rows_here * row_part[:, None] * col_scale[None, :]
    large_sum = jnp.sum(scaled_rows * scaled_rows)
    small_total, large_total = lax.psum((small_sum, large_sum), ("dp", "mp"))
    norm_pair = jnp.stack([small_total, large_total]) / (K * COUT)
    return (output, left_factor, right_factor, norm_pair)


def flip(bit, by):
    return 1 - bit if by else bit


def halves(value):
    high = value.astype(BF16)
    return high, (value - high.astype(F32)).astype(BF16)


def dot3(a, b, dims):
    a_high, a_low = a
    b_high, b_low = b
    dot = functools.partial(
        lax.dot_general, dimension_numbers=(dims, ((), ())), preferred_element_type=F32
    )
    return dot(a_high, b_high) + (dot(a_high, b_low) + dot(a_low, b_high))


def kernel(
    patches_in, weight_in, bias_in, cot, row_scale, col_scale, output_out, left, right, norms,
    grad, got_x, got_p, got_i, column, lparts, lcore, ly, bcol, racc, rgot, nown, ngot, fsplit,
    s_x, r_x, s_p, r_p, s_i, r_i,
    s_gx, r_gx, s_gp, s_gi, r_g,
    s_lc, r_lc, s_ly, r_ly, s_b1, s_b2, r_b, s_r, r_r, s_n, r_n,
    patches, weight, output, load, w_load, o_store,
    bsum, bp, bi, bx, s_bp, r_bp, s_bi, r_bi, s_bx, r_bx,
):
    d, m = lax.axis_index("dp"), lax.axis_index("mp")
    x, z = d % 2, d // 2
    z0, z1 = z % 2, z // 2
    c, y = m % 2, m // 2
    zs = (z, z + 1 - 2 * z0, 2 - z1, 3 - 3 * z1)
    px = (d + 1 - 2 * x, m)
    pz = (zs[1] * 2 + x, m)
    pi = ((3 - z) * 2 + x, m)
    pc = (d, m + 1 - 2 * c)
    py = (d, m + 2 - 4 * y)
    inner = (z0 + z1) % 2 == 1
    outer = (z0 + z1) % 2 == 0
    size = rgot.shape[1]
    half = rgot.shape[0]

    def strip_at(k, other):
        return zs[k] * 2 + (1 - x if other else x)

    def strip(k, other):
        return pl.ds(pl.multiple_of(strip_at(k, other) * size, size), size)

    low = bx.shape[0]
    top = size - low
    head = pl.ds(0, top)

    def upper(k, other):
        return pl.ds(pl.multiple_of(strip_at(k, other) * size, size), top)

    def lower(k, other):
        return pl.ds(pl.multiple_of(strip_at(k, other) * size + top, low), low)

    def copy(src, dst, send, recv, to):
        return pltpu.make_async_remote_copy(
            src_ref=src, dst_ref=dst, send_sem=send, recv_sem=recv, device_id=to, device_id_type=MESH
        )

    barrier = pltpu.get_barrier_semaphore()
    for to in (px, pz, pi, pc, py):
        pl.semaphore_signal(barrier, inc=1, device_id=to, device_id_type=MESH)
    ORDER = (3, 2, 1, 0)
    loads = {}
    for o in (1, 0):
        for k in ORDER:
            rows = strip(k, o)
            loads[k, o] = pltpu.make_async_copy(
                patches_in.at[:, rows], patches.at[:, rows], load.at[2 * k + o]
            )
            loads[k, o].start()
    weight_load = pltpu.make_async_copy(weight_in, weight, w_load)
    weight_load.start()
    nown[...] = jnp.zeros_like(nown)
    pl.semaphore_wait(barrier, 5)
    bias = bias_in[...].reshape(1, size)
    col_row = col_scale[...].reshape(1, size)
    col_square = col_row * col_row

    def folded(value, at):
        square = value * value * col_square
        total = jnp.zeros((1, size), F32)
        for b in range(size // 128):
            scale = row_scale[pl.ds(at * (size // 128) + b, 1), :]
            total += dot3(
                halves(scale * scale), halves(square[b * 128:(b + 1) * 128]), ((1,), (0,))
            )
        return total

    def make_grad(k, other):
        rows = strip(k, other)
        loads[k, other].wait()
        grad[rows, :] = lax.dot_general(
            patches[:, rows], cot[...], (((0,), (0,)), ((), ())), preferred_element_type=F32
        )

    xc = [copy(grad.at[upper(k, 1)], got_x.at[k, head], s_x.at[k], r_x.at[k], px) for k in range(4)]
    for k in ORDER:
        make_grad(k, 1)
        xc[k].start()
    for k in ORDER:
        make_grad(k, 0)

    weight_load.wait()

    for k in range(4):
        for o in range(2):
            bsum[k, o] = grad[lower(k, o), :]
    b_p = {k: copy(bsum.at[k], bp.at[k - 1], s_bp.at[k - 1], r_bp.at[k - 1], pz) for k in (1, 2, 3)}
    b_i = {k: copy(bsum.at[k], bi.at[k - 2], s_bi.at[k - 2], r_bi.at[k - 2], pi) for k in (2, 3)}
    b_x = copy(bsum.at[0, 1], bx, s_bx, r_bx, px)

    @pl.when(outer)
    def _():
        for k in ORDER[:3]:
            b_p[k].start()

    def small_norm(s, _):
        rows = pl.ds(pl.multiple_of(s * size, size), size)
        nown[0, 0:1, :] += folded(grad[rows, :], s)
        return 0

    lax.fori_loop(0, 8, small_norm, 0)

    def out_tile(i, _):
        rows = pl.ds(pl.multiple_of(i * 128, 128), 128)
        value = jnp.dot(patches[rows, :], weight[...], preferred_element_type=F32) + bias
        output[rows, :] = value.astype(BF16)
        return 0

    def out_tiles(a, b):
        lax.fori_loop(a, b, out_tile, 0)

    tiles = patches.shape[0] // 128
    cuts = [0, tiles // 3, 2 * (tiles // 3), tiles]

    @pl.when(inner)
    def _():
        for k in (3, 2):
            b_p[k].wait_recv()
            bsum[k] += bp[k - 1]
            b_i[k].start()
        b_i[3].wait_recv()
        bsum[1] += bi[1]
        b_p[1].start()

    to_p = {
        k: copy(got_x.at[k, head], got_p.at[k - 1], s_p.at[k - 1], r_p.at[k - 1], pz) for k in (1, 2, 3)
    }
    to_i = {
        k: copy(got_x.at[k, head], got_i.at[k - 2], s_i.at[k - 2], r_i.at[k - 2], pi) for k in (2, 3)
    }
    for k in ORDER:
        xc[k].wait_recv()
        got_x[k, head] += grad[upper(k, 0), :]
        if k == 3:
            b_p[1].wait_recv()
            bsum[0] += bp[0]

            @pl.when(inner)
            def _():
                b_i[2].wait_recv()
                bsum[0] += bi[0]

            b_x.start()
        if k >= 1:

            @pl.when(outer)
            def _():
                to_p[k].start()

        if k >= 2:

            @pl.when(inner)
            def _():
                to_p[k].wait_recv()
                got_x[k, head] += got_p[k - 1]
                to_i[k].start()

            out_tiles(cuts[3 - k], cuts[4 - k])
        if k == 1:

            @pl.when(inner)
            def _():
                to_i[3].wait_recv()
                got_x[1, head] += got_i[1]
                to_p[1].start()

            out_tiles(cuts[2], cuts[3])
            out_copy = pltpu.make_async_copy(output, output_out, o_store)
            out_copy.start()
    to_p[1].wait_recv()
    got_x[0, head] += got_p[0]

    @pl.when(inner)
    def _():
        to_i[2].wait_recv()
        got_x[0, head] += got_i[0]

    b_x.wait_recv()
    got_x[0, pl.ds(top, low)] = bsum[0, 0] + bx[...]
    own = strip(0, 0)
    column[own, :] = got_x[0]

    def col(k, other):
        return column.at[strip(k, other)]

    def pass_on(k, recv, send, to):
        return copy(col(k, 0), col(k, 0), send, r_g.at[recv], to)

    gp = [pass_on((0, 2, 3)[j], j + 1, s_gp.at[j], pz) for j in range(3)]
    gi = [pass_on(j, j + 2, s_gi.at[j], pi) for j in range(2)]
    g_in = [pass_on(k, k, s_gp.at[0], pz) for k in range(4)]
    gx = [copy(col(k, 0), col(k, 0), s_gx.at[k], r_gx.at[k], px) for k in range(4)]
    gx_in = [copy(col(k, 1), col(k, 1), s_gx.at[k], r_gx.at[k], px) for k in range(4)]
    units = [(k, o) for k in range(4) for o in range(2)]
    lcc = {
        (k, o): copy(
            lparts.at[k, o], lcore.at[k, o], s_lc.at[2 * k + o], r_lc.at[2 * k + o], pc
        )
        for k, o in units
    }
    lyc = {(k, o): copy(lparts.at[k, o], ly.at[o], s_ly.at[o], r_ly.at[o], py) for k, o in units}
    b_core = [copy(col(k, 0), bcol.at[k], s_b1.at[k], r_b.at[k], pc) for k in range(4)]
    b_y = [copy(col(k, 0), bcol.at[k], s_b2.at[k], r_b.at[k], py) for k in range(4)]
    b_on = [copy(bcol.at[k], bcol.at[k], s_b1.at[k], r_b.at[k], pc) for k in range(4)]
    source = m == z
    relay = py[1] == z

    def arrive(k):
        if k >= 1:
            g_in[k].wait_recv()
        gx[k].start()
        if k == 0:
            gp[0].start()

        @pl.when(inner)
        def _():
            if k <= 1:
                gi[k].start()
            else:
                gp[k - 1].start()

        @pl.when(source)
        def _():
            b_y[k].start()
            b_core[k].start()

    arrive(0)
    high, low = halves(got_x[0])
    fsplit[0] = high
    fsplit[1] = low
    nown[0, 8:9, :] = folded(got_x[0], strip_at(0, 0))
    n_to = (pc, py, pz, pi, px)
    nc = [copy(nown.at[i], ngot.at[i], s_n.at[i], r_n.at[i], n_to[i]) for i in range(5)]
    nc[0].start()
    waiting = []

    def collect():
        if not waiting:
            return
        k, o = waiting.pop(0)

        @pl.when(zs[k] % 2 == c)
        def _():
            lcc[k, o].wait_recv()
            lparts[k, o] += lcore[k, o]

            @pl.when(zs[k] // 2 != y)
            def _():
                lyc[k, o].start()

    def left_unit(k, o):
        if o:
            gx_in[k].wait_recv()
        lparts[k, o] = dot3((fsplit[0], fsplit[1]), halves(column[strip(k, o), :]), ((1,), (1,)))

        @pl.when(zs[k] % 2 != c)
        def _():
            lcc[k, o].start()

        collect()
        waiting.append((k, o))

    def right_unit(k):
        @pl.when(source)
        def _():
            bcol[k] = column[strip(k, 0), :]

        @pl.when(jnp.logical_not(source))
        def _():
            b_core[k].wait_recv()

        @pl.when(relay)
        def _():
            b_on[k].start()

        value = dot3(halves(bcol[k]), halves(column[strip(k, 0), :]), ((0,), (0,)))
        if k == 0:
            racc[...] = value
        else:
            racc[...] += value

    def norm_step(i):
        nc[i].wait_recv()
        nown[i + 1] = nown[i] + ngot[i]
        nc[i + 1].start()

    left_unit(0, 0)
    for k in range(1, 4):
        arrive(k)
        left_unit(k, 0)
        left_unit(k - 1, 1)
        collect()
        right_unit(k - 1)
        norm_step(k - 1)
    left_unit(3, 1)
    norm_step(3)
    right_unit(3)
    rc = copy(
        racc.at[pl.ds(pl.multiple_of((1 - x) * half, half), half)], rgot, s_r, r_r, px
    )
    rc.start()
    collect()
    nc[4].wait_recv()
    both = nown[4] + ngot[4]
    norms[0] = jnp.sum(both[0:8]) / (K * COUT)
    norms[1] = jnp.sum(both[8:16]) / (K * COUT)
    at_k = 0
    for k in range(1, 4):
        at_k = at_k + k * (zs[k] == m).astype(jnp.int32)
    for o in range(2):
        lyc[0, o].wait_recv()
        at = pl.multiple_of((1 - x if o else x) * size, size)
        left[:, pl.ds(at, size)] = (lparts[at_k, o] + ly[o]) * (1.0 / COUT)
    rc.wait_recv()
    right[...] = (racc[pl.ds(pl.multiple_of(x * half, half), half), :] + rgot[...]) * (1.0 / K)

    out_copy.wait()
    for one in (*xc, b_x, b_p[1], to_p[1], gp[0], *gx, rc, *nc, lyc[0, 0], lyc[0, 1]):
        one.wait_send()

    @pl.when(outer)
    def _():
        to_p[2].wait_send()
        to_p[3].wait_send()
        b_p[2].wait_send()
        b_p[3].wait_send()

    @pl.when(inner)
    def _():
        for one in (b_i[2], b_i[3], to_i[2], to_i[3], gp[1], gp[2], *gi):
            one.wait_send()

    for k in range(4):

        @pl.when(zs[k] % 2 != c)
        def _():
            lcc[k, 0].wait_send()
            lcc[k, 1].wait_send()

        @pl.when(source)
        def _():
            b_y[k].wait_send()
            b_core[k].wait_send()

        @pl.when(relay)
        def _():
            b_on[k].wait_send()


def fused(patches, weight, conv_bias, cotangent, row_scale, col_scale):
    rows, width = patches.shape
    cols = cotangent.shape[1]
    size = width // 8
    low = size // 6
    vmem = pl.BlockSpec(memory_space=pltpu.VMEM)
    hbm = pl.BlockSpec(memory_space=pl.ANY)
    dma = pltpu.SemaphoreType.DMA
    one, four = dma, dma((4,))
    return pl.pallas_call(
        kernel,
        out_shape=(
            jax.ShapeDtypeStruct((rows, cols), BF16),
            jax.ShapeDtypeStruct((size, width // 4), F32),
            jax.ShapeDtypeStruct((cols // 2, cols), F32),
            jax.ShapeDtypeStruct((2,), F32),
        ),
        in_specs=[hbm, hbm, vmem, vmem, vmem, vmem],
        out_specs=(hbm, vmem, vmem, pl.BlockSpec(memory_space=pltpu.SMEM)),
        scratch_shapes=[
            pltpu.VMEM((width, cols), F32),
            pltpu.VMEM((4, size, cols), F32),
            pltpu.VMEM((3, size - low, cols), F32),
            pltpu.VMEM((2, size - low, cols), F32),
            pltpu.VMEM((width, cols), F32),
            pltpu.VMEM((4, 2, size, size), F32),
            pltpu.VMEM((4, 2, size, size), F32),
            pltpu.VMEM((2, size, size), F32),
            pltpu.VMEM((4, size, cols), F32),
            pltpu.VMEM((cols, cols), F32),
            pltpu.VMEM((cols // 2, cols), F32),
            pltpu.VMEM((5, 16, cols), F32),
            pltpu.VMEM((5, 16, cols), F32),
            pltpu.VMEM((2, size, cols), BF16),
            four, four, dma((3,)), dma((3,)), dma((2,)), dma((2,)),
            four, four, dma((3,)), dma((2,)), four,
            dma((8,)), dma((8,)), dma((2,)), dma((2,)), four, four, four, one, one,
            dma((5,)), dma((5,)),
            pltpu.VMEM((rows, width), BF16),
            pltpu.VMEM((width, cols), BF16),
            pltpu.VMEM((rows, cols), BF16),
            dma((8,)), one, one,
            pltpu.VMEM((4, 2, low, cols), F32),
            pltpu.VMEM((3, 2, low, cols), F32),
            pltpu.VMEM((2, 2, low, cols), F32),
            pltpu.VMEM((low, cols), F32),
            dma((3,)), dma((3,)), dma((2,)), dma((2,)), one, one,
        ],
        compiler_params=pltpu.CompilerParams(
            collective_id=0, has_side_effects=True, vmem_limit_bytes=60 * 1024 * 1024
        ),
    )(
        patches, weight, conv_bias, cotangent, row_scale.reshape(-1, 128), col_scale
    )


def solution(mesh):
    in_specs = (P("dp", None), P(None, "mp"), P("mp"), P("dp", "mp"), P(), P("mp"))
    out_specs = (P("dp", "mp"), P("dp", "mp"), P("dp", "mp"), P())
    body = fused if (mesh.shape["dp"], mesh.shape["mp"]) == (8, 4) else shards
    return jax.shard_map(body, mesh=mesh, in_specs=in_specs, out_specs=out_specs, check_vma=False)
```
